32 devices in a mesh: expert: 4 (over x, core), shard: 8 (over z, y).
Axes of the slice: x: 2, y: 2, z: 4, core: 2. Of those that a mesh axis runs over, the one named last changes fastest.
Arguments:
- tokens_in: bfloat16 [1024, 4096], P(('expert', 'shard')), may hold values from -6 to 6
- out_grad: bfloat16 [1024, 2, 8192], P(('expert', 'shard')), may hold values from -6 to 6
- expert_ids: int32 [1024, 2], P(('expert', 'shard')), may hold values from 0 to 3, all different within a row; in each aligned block of 32 rows (0 to 31, 32 to 63, ...) at most 20 rows name the same one
- d_levels: int32 [4, 16], P('expert'), may hold values from 0 to 7
- f_levels: int32 [4, 32], P('expert', 'shard'), may hold values from 0 to 7
Outputs:
- ascent: bfloat16 [4, 4096, 8192], P('expert', None, 'shard')
The draws below stay inside these ranges and needn't reach their ends.
Inputs may be any that keep to these rules, and one draw needn't show every extreme that they name: `expert_ids`: each token names two different experts; among the 64 entries of one device no expert is named more than 20 times, and 20 is reached on some device; every expert is named somewhere.
All inputs are finite; a program needn't handle non-finite values.
Results may differ from the reference program's by a relative error of at most 0.001.
Values may be sent and summed in bfloat16 or wider, within the bound.
A program may use at most 128 MiB of HBM per device.

```python
import math
import jax
import jax.numpy as jnp
import numpy as np
from jax import lax

D = 4096
FF = 8192
BLK = 256
TOK_DEV = 32
EXPERTS = 4
CAP = 20
TOKENS = 1024
N_EXPERT = 4
N_SHARD = 8


def place_ends(values, own_key, least, high):
    longest = values.shape.index(max(values.shape))
    spots = []
    for shift in (0, 1):
        where = [jax.random.randint(jax.random.fold_in(own_key, axis), (), 0, length) for axis, length in enumerate(values.shape)]
        where[longest] = (where[longest] + shift) % values.shape[longest]
        spots.append(tuple(where))
    return values.at[spots[0]].set(least).at[spots[1]].set(high)


def block_scale(rng, dims, cuts, low, high):
    def one(dim, parts):
        steps = jax.random.uniform(jax.random.fold_in(jax.random.fold_in(rng, 6), dim), (parts,), jnp.float32, low / len(cuts), high / len(cuts))
        return jnp.repeat(jnp.exp(steps), dims[dim] // parts).reshape((-1,) + (1,) * (len(dims) - dim - 1))

    loudness = one(*cuts[0])
    for cut in cuts[1:]:
        loudness = loudness * one(*cut)
    return loudness


def assign_block(rng, own, number, rows, count, top, reach, lean):
    sequence = jax.random.permutation(rng, count)
    packed, usual = portions_of(count, rows * top, reach, lean, True), portions_of(count, rows * top, reach, lean, False)
    places = jnp.arange(count)

    def named(tallies, turn):
        used = int((tallies > 0).sum())
        fixed = max(1, used // 4)
        moved = fixed + (places - fixed + turn * (used - fixed)) % max(1, count - fixed)
        return jnp.zeros((count,), jnp.int32).at[sequence[jnp.where(places < fixed, places, moved)]].set(jnp.asarray(tallies, jnp.int32))

    tallies = jnp.where(number % 4 == 0, named(packed, number // 4), named(usual, number - number // 4 - 1))
    mixed = jax.random.permutation(jax.random.fold_in(own, 3), count)
    giver, sink = mixed[0:count // 2 * 2:2], mixed[1:count // 2 * 2:2]
    room = jnp.minimum(tallies[giver] - 1, reach - tallies[sink]) // 2
    room = jnp.where((giver == sequence[0]) | (sink == sequence[0]) | (tallies[sink] == 0), 0, jnp.maximum(room, 0))
    moved = jax.random.randint(jax.random.fold_in(own, 4), (count // 2,), 0, 1 << 20) % (room + 1)
    tallies = tallies.at[giver].add(-moved).at[sink].add(moved)
    members = jnp.searchsorted(jnp.cumsum(tallies), jnp.arange(rows * top), side="right").astype(jnp.int32)
    grid = members.reshape(top, rows).T
    grid = grid[jax.random.permutation(jax.random.fold_in(own, 1), rows)]
    turn = jax.random.randint(jax.random.fold_in(own, 2), (rows, 1), 0, top)
    return jnp.take_along_axis(grid, (jnp.arange(top)[None, :] + turn) % top, axis=1)


def portions_of(count, total, bound, slope, full):
    loads = [(1 << 20) // math.isqrt(rank ** slope) + 1 for rank in range(1, count + 1)]
    largest = bound if full else min(bound, max(-(-total // count), total * loads[0] // sum(loads)))
    least = 1 if total - largest >= count - 1 else 0
    counts, spare = [largest] + [least] * (count - 1), total - largest - least * (count - 1)
    while spare > 0:
        movable = [i for i in range(1, count) if counts[i] < largest] or [i for i in range(1, count) if counts[i] < bound]
        whole, remaining = sum([loads[i] for i in movable]), spare
        for i in movable:
            addition = min(bound - counts[i], max(1, remaining * loads[i] // whole), spare)
            counts[i] = counts[i] + addition
            spare = spare - addition
    return np.array(counts)


def normal_values(own_key, shape, scale, bound, shards=(), held_as=jnp.bfloat16):
    values = scale * jax.random.normal(own_key, shape, jnp.float32)
    if shards:
        values = values * block_scale(own_key, shape, shards, -0.22, 0.18)
    return jnp.clip(values, -bound, bound).astype(held_as)


def setup_inputs(seed: int = 0) -> dict:
    splits = jax.random.split(jax.random.key(seed), 6)
    tokens_in = normal_values(splits[0], (TOKENS, D), 1.0, 6.0, ((0, 32),))
    out_grad = normal_values(splits[1], (TOKENS, 2, FF), 1.0, 6.0, ((0, 32),))
    expert_ids_keys = jax.random.split(jax.random.fold_in(splits[2], 1), TOKENS // TOK_DEV)
    expert_ids_turns = jax.random.permutation(jax.random.fold_in(splits[2], 3), TOKENS // TOK_DEV)
    expert_ids = jax.vmap(lambda own, number: assign_block(jax.random.fold_in(splits[2], 2), own, number, TOK_DEV, EXPERTS, 2, CAP, 2))(expert_ids_keys, expert_ids_turns).reshape((TOKENS, 2))
    d_levels = place_ends(jax.random.randint(splits[3], (EXPERTS, D // BLK), 0, 8), jax.random.fold_in(splits[3], 1), 0, 7).astype(jnp.int32)
    f_levels = place_ends(jax.random.randint(splits[4], (EXPERTS, FF // BLK), 0, 8), jax.random.fold_in(splits[4], 1), 0, 7).astype(jnp.int32)
    return {"tokens_in": tokens_in, "out_grad": out_grad, "expert_ids": expert_ids, "d_levels": d_levels, "f_levels": f_levels}


def invert_blocks(blocks):
    lower = jnp.linalg.cholesky(blocks)
    identity = jnp.eye(blocks.shape[-1], dtype=blocks.dtype)
    return jax.vmap(lambda factor: jax.scipy.linalg.cho_solve((factor, True), identity))(lower)

def damping(levels):
    return 0.05 * jnp.exp(0.4 * levels.astype(jnp.float32))

def reference(tokens_in, out_grad, expert_ids, d_levels, f_levels):
    row_limit = N_EXPERT * N_SHARD * CAP
    flat_ids = expert_ids.reshape(-1)
    tok_index = (jnp.arange(2 * TOKENS, dtype=jnp.int32) // 2).astype(jnp.int32)
    grads_flat = out_grad.reshape(2 * TOKENS, FF)
    highest = lax.Precision.HIGHEST

    def per_expert(inputs):
        expert, d_row, f_row = inputs
        chosen = flat_ids == expert
        ordering = jnp.argsort(jnp.where(chosen, 0, 1).astype(jnp.int32), stable=True)[:row_limit].astype(jnp.int32)
        live_rows = chosen[ordering].astype(jnp.bfloat16)
        row_count = jnp.sum(chosen.astype(jnp.float32))
        x_rows = tokens_in[tok_index[ordering]] * live_rows[:, None]
        g_rows = grads_flat[ordering] * live_rows[:, None]
        gradient = jnp.dot(x_rows.T.astype(jnp.float32), g_rows.astype(jnp.float32), preferred_element_type=jnp.float32)
        x_blocks = x_rows.astype(jnp.float32).reshape(row_limit, D // BLK, BLK)
        g_blocks = g_rows.astype(jnp.float32).reshape(row_limit, FF // BLK, BLK)
        identity = jnp.eye(BLK, dtype=jnp.float32)
        cov_a = jnp.einsum('rbi,rbj->bij', x_blocks, x_blocks, precision=highest) / row_count
        cov_a = cov_a + damping(d_row)[:, None, None] * identity
        cov_f = jnp.einsum('rbi,rbj->bij', g_blocks, g_blocks, precision=highest) / row_count
        cov_f = cov_f + damping(f_row)[:, None, None] * identity
        inv_a = invert_blocks(cov_a)
        inv_f = invert_blocks(cov_f)
        left_done = jnp.einsum('bij,bjf->bif', inv_a, gradient.reshape(D // BLK, BLK, FF), precision=highest)
        precond = jnp.einsum('dcj,cjk->dck', left_done.reshape(D, FF // BLK, BLK), inv_f, precision=highest)
        return precond.reshape(D, FF)
    precond = lax.map(per_expert, (jnp.arange(EXPERTS, dtype=jnp.int32), d_levels, f_levels))
    norm_total = jnp.sum(precond * precond)
    ascent_scale = lax.rsqrt(norm_total / (EXPERTS * D * FF) + 1e-06)
    return (precond * ascent_scale).astype(jnp.bfloat16)
```

```python
import functools

import jax
import jax.numpy as jnp
from jax import lax
from jax.experimental import pallas as pl
from jax.experimental.pallas import tpu as pltpu
from jax.sharding import PartitionSpec as P

BLK = 256
HALF = BLK // 2
MARK = 128
NT = (((1,), (1,)), ((), ()))
TN = (((0,), (0,)), ((), ()))


def dot_f32(a, b, dims=(((1,), (0,)), ((), ()))):
    return lax.dot_general(
        a, b, dims, precision=lax.Precision.HIGHEST, preferred_element_type=jnp.float32
    )


def dot_bf16(a, b, dims=(((1,), (0,)), ((), ()))):
    return lax.dot_general(a, b, dims, preferred_element_type=jnp.float32)


def split(value, parts):
    out = []
    for _ in range(parts):
        part = value.astype(jnp.bfloat16)
        out.append(part)
        value = value - part.astype(jnp.float32)
    return out


def gauss_jordan(work, count):
    lanes = lax.broadcasted_iota(jnp.int32, (HALF, HALF), 1)
    lane_row = lax.broadcasted_iota(jnp.int32, (1, HALF), 1)

    def step(j, carry):
        index = jnp.full((HALF, HALF), j, jnp.int32)
        at_pivot = lanes == j
        for b in range(count):
            matrix = work[b]
            row = work[b, pl.ds(j, 1), :]
            column = jnp.take_along_axis(matrix, index, axis=1)
            pivot = jnp.sum(jnp.where(lane_row == j, row, 0.0), axis=1, keepdims=True)
            scaled = jnp.where(lane_row == j, 1.0, row) / pivot
            work[b] = jnp.where(at_pivot, 0.0, matrix) - column * scaled
            work[b, pl.ds(j, 1), :] = scaled
        return carry

    lax.fori_loop(0, HALF, step, 0)


def invert_covariances(rows_ref, damp_ref, count_ref, work, cov, aux):
    count = cov.shape[0]
    eye = (
        lax.broadcasted_iota(jnp.int32, (BLK, BLK), 0)
        == lax.broadcasted_iota(jnp.int32, (BLK, BLK), 1)
    )
    for b in range(count):
        rows = rows_ref[:, b * BLK : (b + 1) * BLK]
        product = dot_bf16(rows, rows, TN) / count_ref[0]
        cov[b] = product + jnp.where(eye, damp_ref[b], 0.0)
        work[b] = cov[b, :HALF, :HALF]
    gauss_jordan(work, count)
    for b in range(count):
        first = work[b]
        upper = cov[b, :HALF, HALF:]
        side = dot_f32(first, upper)
        aux[b] = side
        cov[b, :HALF, :HALF] = first
        work[b] = cov[b, HALF:, HALF:] - dot_f32(upper, side, TN)
    gauss_jordan(work, count)
    for b in range(count):
        last = work[b]
        side = aux[b]
        corner = dot_f32(side, last)
        cov[b, :HALF, :HALF] = cov[b, :HALF, :HALF] + dot_f32(corner, side, NT)
        cov[b, :HALF, HALF:] = -corner
        cov[b, HALF:, :HALF] = -corner.T
        cov[b, HALF:, HALF:] = last


def input_kernel(damp_ref, count_ref, rows_ref, inv_ref, work, aux):
    invert_covariances(rows_ref, damp_ref, count_ref, work, inv_ref, aux)


def hidden_kernel(damp_ref, count_ref, rows_ref, high_ref, low_ref, work, aux, cov):
    invert_covariances(rows_ref, damp_ref, count_ref, work, cov, aux)
    for b in range(cov.shape[0]):
        columns = slice(b * BLK, (b + 1) * BLK)
        rows = rows_ref[:, columns]
        total = sum(dot_bf16(rows, part) for part in reversed(split(cov[b], 3)))
        high_ref[:, columns], low_ref[:, columns] = split(total, 2)


def product_kernel(rows_ref, inv_ref, high_ref, low_ref, out_ref, norm_ref):
    rows = rows_ref[0]
    left = sum(dot_bf16(part, rows, NT) for part in reversed(split(inv_ref[0], 3)))
    left_high, left_low = split(left, 2)
    high = high_ref[...]
    out = dot_bf16(left_high, low_ref[...]) + dot_bf16(left_low, high) + dot_bf16(left_high, high)
    out_ref[...] = out

    @pl.when(pl.program_id(0) == 0)
    def _():
        norm_ref[...] = jnp.zeros_like(norm_ref)

    norm_ref[...] += jnp.sum((out * out).reshape(-1, 8, out.shape[1]), axis=0)


def damping(levels):
    return 0.05 * jnp.exp(0.4 * levels.astype(jnp.float32))


def call_blocks(kernel, damp, row_count, rows, out_shape, with_cov):
    count = damp.shape[0]
    scratch = [pltpu.VMEM((count, HALF, HALF), jnp.float32)] * 2
    if with_cov:
        scratch.append(pltpu.VMEM((count, BLK, BLK), jnp.float32))
    vmem = pl.BlockSpec(memory_space=pltpu.VMEM)
    smem = pl.BlockSpec(memory_space=pltpu.SMEM)
    return pl.pallas_call(
        kernel,
        out_shape=out_shape,
        in_specs=[smem, smem, vmem],
        out_specs=jax.tree.map(lambda _: vmem, out_shape),
        scratch_shapes=scratch,
        compiler_params=pltpu.CompilerParams(vmem_limit_bytes=48 << 20),
        cost_estimate=pl.CostEstimate(flops=20_000_000_000, bytes_accessed=4_000_000, transcendentals=0),
    )(damp, row_count, rows)


def local(tokens_in, out_grad, expert_ids, d_levels, f_levels):
    group_count = lax.axis_size("expert")
    shard_count = lax.axis_size("shard")
    tok_rows = tokens_in.shape[0]
    width = tokens_in.shape[1]
    ff_full = out_grad.shape[2]
    ff_dev = ff_full // shard_count
    width_dev = width // shard_count
    capacity = min(tok_rows, max(2, 5 * tok_rows // (2 * group_count)))
    slot_total = group_count * capacity
    flat_ids = expert_ids.reshape(-1)
    member = (flat_ids[:, None] == jnp.arange(group_count, dtype=jnp.int32)[None, :]).astype(
        jnp.int32
    )
    before = jnp.cumsum(member, axis=0) - member
    ranking = jnp.sum(before * member, axis=1)
    target = flat_ids * capacity + ranking
    dispatch = (jnp.arange(slot_total, dtype=jnp.int32)[:, None] == target[None, :]).astype(
        jnp.bfloat16
    )
    per_token = jnp.sum(
        dispatch.reshape(slot_total, tok_rows, 2).astype(jnp.float32), axis=2
    ).astype(jnp.bfloat16)
    x_send = jnp.dot(per_token, tokens_in, preferred_element_type=jnp.float32).astype(jnp.bfloat16)
    g_send = jnp.dot(
        dispatch, out_grad.reshape(2 * tok_rows, ff_full), preferred_element_type=jnp.float32
    ).astype(jnp.bfloat16)
    valid_slot = jnp.sum(dispatch.astype(jnp.float32), axis=1).astype(jnp.bfloat16)
    send = jnp.concatenate(
        (
            x_send.reshape(group_count, capacity, shard_count, width_dev),
            g_send.reshape(group_count, capacity, shard_count, ff_dev),
            jnp.broadcast_to(
                valid_slot.reshape(group_count, capacity, 1, 1),
                (group_count, capacity, shard_count, MARK),
            ),
        ),
        axis=3,
    )
    send = send.transpose(0, 2, 1, 3).reshape(group_count * shard_count, capacity, -1)
    rows = lax.all_to_all(send, ("expert", "shard"), split_axis=0, concat_axis=0, tiled=True)
    rows = rows.reshape(-1, rows.shape[2])
    own_x = rows[:, :width_dev]
    rows_g = rows[:, width_dev : width_dev + ff_dev]
    row_count = jnp.sum(rows[:, width_dev + ff_dev].astype(jnp.float32)).reshape(1)
    row_total = rows.shape[0]
    rows_x = lax.all_gather(own_x, "shard", axis=0)

    own_blocks = width_dev // BLK
    first_block = lax.axis_index("shard") * own_blocks
    own_levels = lax.dynamic_slice_in_dim(d_levels[0], first_block, own_blocks, 0)
    inv_a = call_blocks(
        input_kernel,
        damping(own_levels),
        row_count,
        own_x,
        jax.ShapeDtypeStruct((own_blocks, BLK, BLK), jnp.float32),
        False,
    )
    inv_a = lax.all_gather(inv_a, "shard", axis=0, tiled=True)
    half = jax.ShapeDtypeStruct((row_total, ff_dev), jnp.bfloat16)
    g_high, g_low = call_blocks(
        hidden_kernel, damping(f_levels[0]), row_count, rows_g, (half, half), True
    )
    blocks = width // BLK
    whole = pl.BlockSpec((row_total, ff_dev), lambda b: (0, 0))
    precond, squares = pl.pallas_call(
        product_kernel,
        grid=(blocks,),
        out_shape=(
            jax.ShapeDtypeStruct((width, ff_dev), jnp.float32),
            jax.ShapeDtypeStruct((8, ff_dev), jnp.float32),
        ),
        in_specs=[
            pl.BlockSpec((1, row_total, BLK), lambda b: (b // own_blocks, 0, b % own_blocks)),
            pl.BlockSpec((1, BLK, BLK), lambda b: (b, 0, 0)),
            whole,
            whole,
        ],
        out_specs=(
            pl.BlockSpec((BLK, ff_dev), lambda b: (b, 0)),
            pl.BlockSpec((8, ff_dev), lambda b: (0, 0)),
        ),
        compiler_params=pltpu.CompilerParams(
            dimension_semantics=("arbitrary",), vmem_limit_bytes=48 << 20
        ),
        cost_estimate=pl.CostEstimate(
            flops=6 * row_total * width * ff_dev, bytes_accessed=4 * width * ff_dev, transcendentals=0
        ),
    )(rows_x, inv_a, g_high, g_low)
    norm_total = lax.psum(jnp.sum(squares), ("expert", "shard"))
    ascent_scale = lax.rsqrt(norm_total / (group_count * width * ff_full) + 1e-06)
    return (precond * ascent_scale).astype(jnp.bfloat16)[None]


def solution(mesh):
    return jax.shard_map(
        local,
        mesh=mesh,
        in_specs=(
            P(("expert", "shard"), None),
            P(("expert", "shard"), None, None),
            P(("expert", "shard"), None),
            P("expert", None),
            P("expert", "shard"),
        ),
        out_specs=P("expert", None, "shard"),
        check_vma=False,
    )
```

```python
import functools

import jax
import jax.numpy as jnp
from jax import lax
from jax.experimental import pallas as pl
from jax.experimental.pallas import tpu as pltpu
from jax.sharding import PartitionSpec as P

BLK = 256
HALF = BLK // 2
MARK = 128
NT = (((1,), (1,)), ((), ()))
TN = (((0,), (0,)), ((), ()))


def dot_f32(a, b, dims=(((1,), (0,)), ((), ()))):
    return lax.dot_general(
        a, b, dims, precision=lax.Precision.HIGHEST, preferred_element_type=jnp.float32
    )


def dot_bf16(a, b, dims=(((1,), (0,)), ((), ()))):
    return lax.dot_general(a, b, dims, preferred_element_type=jnp.float32)


def split(value, parts):
    out = []
    for _ in range(parts):
        part = value.astype(jnp.bfloat16)
        out.append(part)
        value = value - part.astype(jnp.float32)
    return out


def gauss_jordan(work, count):
    lanes = lax.broadcasted_iota(jnp.int32, (HALF, HALF), 1)
    lane_row = lax.broadcasted_iota(jnp.int32, (1, HALF), 1)

    def step(j, carry):
        index = jnp.full((HALF, HALF), j, jnp.int32)
        at_pivot = lanes == j
        matrices = [work[b] for b in range(count)]
        rows = [work[b, pl.ds(j, 1), :] for b in range(count)]
        pivots = [
            jnp.sum(jnp.where(lane_row == j, row, 0.0), axis=1, keepdims=True) for row in rows
        ]
        columns = [jnp.take_along_axis(matrix, index, axis=1) for matrix in matrices]
        scaled = [
            jnp.where(lane_row == j, 1.0, row) / pivot for row, pivot in zip(rows, pivots)
        ]
        updated = [
            jnp.where(at_pivot, 0.0, matrix) - column * row
            for matrix, column, row in zip(matrices, columns, scaled)
        ]
        for b in range(count):
            work[b] = updated[b]
        for b in range(count):
            work[b, pl.ds(j, 1), :] = scaled[b]
        return carry

    lax.fori_loop(0, HALF, step, 0)


def invert_covariances(rows_ref, damp_ref, count_ref, work, cov, aux):
    count = cov.shape[0]
    eye = (
        lax.broadcasted_iota(jnp.int32, (BLK, BLK), 0)
        == lax.broadcasted_iota(jnp.int32, (BLK, BLK), 1)
    )
    for b in range(count):
        rows = rows_ref[:, b * BLK : (b + 1) * BLK]
        product = dot_bf16(rows, rows, TN) / count_ref[0]
        cov[b] = product + jnp.where(eye, damp_ref[b], 0.0)
        work[b] = cov[b, :HALF, :HALF]
    gauss_jordan(work, count)
    for b in range(count):
        first = work[b]
        upper = cov[b, :HALF, HALF:]
        side = dot_f32(first, upper)
        aux[b] = side
        cov[b, :HALF, :HALF] = first
        work[b] = cov[b, HALF:, HALF:] - dot_f32(upper, side, TN)
    gauss_jordan(work, count)
    for b in range(count):
        last = work[b]
        side = aux[b]
        corner = dot_f32(side, last)
        cov[b, :HALF, :HALF] = cov[b, :HALF, :HALF] + dot_f32(corner, side, NT)
        cov[b, :HALF, HALF:] = -corner
        cov[b, HALF:, :HALF] = -corner.T
        cov[b, HALF:, HALF:] = last


def input_kernel(damp_ref, count_ref, rows_ref, inv_ref, work, aux):
    invert_covariances(rows_ref, damp_ref, count_ref, work, inv_ref, aux)


def hidden_kernel(damp_ref, count_ref, rows_ref, high_ref, low_ref, work, aux, cov):
    invert_covariances(rows_ref, damp_ref, count_ref, work, cov, aux)
    for b in range(cov.shape[0]):
        columns = slice(b * BLK, (b + 1) * BLK)
        rows = rows_ref[:, columns]
        total = sum(dot_bf16(rows, part) for part in reversed(split(cov[b], 3)))
        high_ref[:, columns], low_ref[:, columns] = split(total, 2)


def product_kernel(rows_ref, inv_ref, high_ref, low_ref, out_ref, norm_ref):
    rows = rows_ref[0]
    left = sum(dot_bf16(part, rows, NT) for part in reversed(split(inv_ref[0], 3)))
    left_high, left_low = split(left, 2)
    high = high_ref[...]
    out = dot_bf16(left_high, low_ref[...]) + dot_bf16(left_low, high) + dot_bf16(left_high, high)
    out_ref[...] = out

    @pl.when(pl.program_id(0) == 0)
    def _():
        norm_ref[...] = jnp.zeros_like(norm_ref)

    norm_ref[...] += jnp.sum((out * out).reshape(-1, 8, out.shape[1]), axis=0)


def damping(levels):
    return 0.05 * jnp.exp(0.4 * levels.astype(jnp.float32))


def call_blocks(kernel, damp, row_count, rows, out_shape, with_cov):
    count = damp.shape[0]
    scratch = [pltpu.VMEM((count, HALF, HALF), jnp.float32)] * 2
    if with_cov:
        scratch.append(pltpu.VMEM((count, BLK, BLK), jnp.float32))
    vmem = pl.BlockSpec(memory_space=pltpu.VMEM)
    smem = pl.BlockSpec(memory_space=pltpu.SMEM)
    return pl.pallas_call(
        kernel,
        out_shape=out_shape,
        in_specs=[smem, smem, vmem],
        out_specs=jax.tree.map(lambda _: vmem, out_shape),
        scratch_shapes=scratch,
        compiler_params=pltpu.CompilerParams(vmem_limit_bytes=48 << 20),
        cost_estimate=pl.CostEstimate(flops=20_000_000_000, bytes_accessed=4_000_000, transcendentals=0),
    )(damp, row_count, rows)


def local(tokens_in, out_grad, expert_ids, d_levels, f_levels):
    group_count = lax.axis_size("expert")
    shard_count = lax.axis_size("shard")
    tok_rows = tokens_in.shape[0]
    width = tokens_in.shape[1]
    ff_full = out_grad.shape[2]
    ff_dev = ff_full // shard_count
    width_dev = width // shard_count
    capacity = min(tok_rows, max(2, 5 * tok_rows // (2 * group_count)))
    slot_total = group_count * capacity
    flat_ids = expert_ids.reshape(-1)
    member = (flat_ids[:, None] == jnp.arange(group_count, dtype=jnp.int32)[None, :]).astype(
        jnp.int32
    )
    before = jnp.cumsum(member, axis=0) - member
    ranking = jnp.sum(before * member, axis=1)
    target = flat_ids * capacity + ranking
    dispatch = (jnp.arange(slot_total, dtype=jnp.int32)[:, None] == target[None, :]).astype(
        jnp.bfloat16
    )
    per_token = jnp.sum(
        dispatch.reshape(slot_total, tok_rows, 2).astype(jnp.float32), axis=2
    ).astype(jnp.bfloat16)
    x_send = jnp.dot(per_token, tokens_in, preferred_element_type=jnp.float32).astype(jnp.bfloat16)
    g_send = jnp.dot(
        dispatch, out_grad.reshape(2 * tok_rows, ff_full), preferred_element_type=jnp.float32
    ).astype(jnp.bfloat16)
    valid_slot = jnp.sum(dispatch.astype(jnp.float32), axis=1).astype(jnp.bfloat16)
    send = jnp.concatenate(
        (
            x_send.reshape(group_count, capacity, shard_count, width_dev),
            g_send.reshape(group_count, capacity, shard_count, ff_dev),
            jnp.broadcast_to(
                valid_slot.reshape(group_count, capacity, 1, 1),
                (group_count, capacity, shard_count, MARK),
            ),
        ),
        axis=3,
    )
    send = send.transpose(0, 2, 1, 3).reshape(group_count * shard_count, capacity, -1)
    rows = lax.all_to_all(send, ("expert", "shard"), split_axis=0, concat_axis=0, tiled=True)
    rows = rows.reshape(-1, rows.shape[2])
    own_x = rows[:, :width_dev]
    rows_g = rows[:, width_dev : width_dev + ff_dev]
    row_count = jnp.sum(rows[:, width_dev + ff_dev].astype(jnp.float32)).reshape(1)
    row_total = rows.shape[0]
    rows_x = lax.all_gather(own_x, "shard", axis=0)

    own_blocks = width_dev // BLK
    first_block = lax.axis_index("shard") * own_blocks
    own_levels = lax.dynamic_slice_in_dim(d_levels[0], first_block, own_blocks, 0)
    inv_a = call_blocks(
        input_kernel,
        damping(own_levels),
        row_count,
        own_x,
        jax.ShapeDtypeStruct((own_blocks, BLK, BLK), jnp.float32),
        False,
    )
    inv_a = lax.all_gather(inv_a, "shard", axis=0, tiled=True)
    half = jax.ShapeDtypeStruct((row_total, ff_dev), jnp.bfloat16)
    g_high, g_low = call_blocks(
        hidden_kernel, damping(f_levels[0]), row_count, rows_g, (half, half), True
    )
    blocks = width // BLK
    whole = pl.BlockSpec((row_total, ff_dev), lambda b: (0, 0))
    precond, squares = pl.pallas_call(
        product_kernel,
        grid=(blocks,),
        out_shape=(
            jax.ShapeDtypeStruct((width, ff_dev), jnp.float32),
            jax.ShapeDtypeStruct((8, ff_dev), jnp.float32),
        ),
        in_specs=[
            pl.BlockSpec((1, row_total, BLK), lambda b: (b // own_blocks, 0, b % own_blocks)),
            pl.BlockSpec((1, BLK, BLK), lambda b: (b, 0, 0)),
            whole,
            whole,
        ],
        out_specs=(
            pl.BlockSpec((BLK, ff_dev), lambda b: (b, 0)),
            pl.BlockSpec((8, ff_dev), lambda b: (0, 0)),
        ),
        compiler_params=pltpu.CompilerParams(
            dimension_semantics=("arbitrary",), vmem_limit_bytes=48 << 20
        ),
        cost_estimate=pl.CostEstimate(
            flops=6 * row_total * width * ff_dev, bytes_accessed=4 * width * ff_dev, transcendentals=0
        ),
    )(rows_x, inv_a, g_high, g_low)
    norm_total = lax.psum(jnp.sum(squares), ("expert", "shard"))
    ascent_scale = lax.rsqrt(norm_total / (group_count * width * ff_full) + 1e-06)
    return (precond * ascent_scale).astype(jnp.bfloat16)[None]


def solution(mesh):
    return jax.shard_map(
        local,
        mesh=mesh,
        in_specs=(
            P(("expert", "shard"), None),
            P(("expert", "shard"), None, None),
            P(("expert", "shard"), None),
            P("expert", None),
            P("expert", "shard"),
        ),
        out_specs=P("expert", None, "shard"),
        check_vma=False,
    )
```
